32 devices in a mesh: groups: 2 (over x), seq: 16 (over z, y, core), sub: 1.
Axes of the slice: x: 2, y: 2, z: 4, core: 2. Of those that a mesh axis runs over, the one named last changes fastest.
Arguments:
- hidden_input: bfloat16 [16384, 4096], P(('groups', 'seq')), parts along dimension 0, may hold values from -4 to 4
- norm_gain_vector: bfloat16 [4096], replicated, may hold values from 0.099609375 to 1.8984375
- query_weight: bfloat16 [4096, 2048], P('seq', 'sub'), may hold values from -0.109375 to 0.109375
- key_value_weight: bfloat16 [4096, 2, 512], P('seq', None, 'sub'), may hold values from -0.109375 to 0.109375
- output_weight: bfloat16 [2048, 4096], P('sub', 'seq'), may hold values from -0.125 to 0.125
- adapter_input_down: bfloat16 [32, 4096, 192], P('seq'), may hold values from -0.09375 to 0.09375
- adapter_query_up: bfloat16 [32, 64, 2048], P('seq', None, 'sub'), may hold values from -0.75 to 0.75
- adapter_key_value_up: bfloat16 [32, 2, 64, 512], P('seq', None, None, 'sub'), may hold values from -0.75 to 0.75
- adapter_output_down: bfloat16 [32, 2048, 64], P('seq', 'sub'), may hold values from -0.125 to 0.125
- adapter_output_up: bfloat16 [32, 64, 4096], P('seq', None, 'sub'), may hold values from -0.75 to 0.75
- request_lengths: int32 [8], P('groups'), parts along dimension 0, may hold values from 1 to 4608, 8192 in all
- request_adapter: int32 [8], P('groups'), parts along dimension 0, may hold values from 0 to 31
- adapter_table_slot: int32 [32], replicated, may hold values from 0 to 31, each once
Outputs:
- block_out: bfloat16 [16384, 4096], P(('groups', 'seq'), 'sub'), parts along dimension 0
The draws below stay inside these ranges and needn't reach their ends.
There are 2 independent parts, one for each index of `groups`. The reference program is written for one: setup_inputs(seed, part) draws one part's arguments, and reference() takes and returns one part's arrays. A program takes and returns all parts, laid end to end along the dimension named above; an argument that names none is the same for every part. Nothing has to cross between parts.
Inputs may be any that keep to these rules, and one draw needn't show every extreme that they name: `request_lengths`: the lengths add up to 8192; the longest request has exactly 4608 tokens. `request_adapter`: several requests may name the same adapter. `adapter_table_slot`: each slot holds one adapter.
All inputs are finite; a program needn't handle non-finite values.
Results may differ from the reference program's by a relative error of at most 0.013.
The reference program's roundings to bfloat16 on the way count: a program that leaves them out, or rounds other values in their place, can miss the bound.
Values may be sent and summed in bfloat16 or wider, within the bound.
No kernel may reach another device: no remote copies, remote signals or barrier semaphores. Data moves between devices by JAX's collectives and lax.ppermute only.
A program may use at most 448 MiB of HBM per device.

```python
import math
import jax
import jax.numpy as jnp
import numpy as np
from jax import lax

MODEL_WIDTH = 4096
QUERY_HEADS = 16
KEY_VALUE_HEADS = 4
HEAD_WIDTH = 128
ADAPTER_RANK = 64
WINDOW = 4096
REQS = 4
WINDOW_TOKENS = 8192
ADAPTER_COUNT = 32
LONGEST = 4608


sink_share = 1.0 / 32.0


def sink_pattern():
    column_index = jnp.arange(MODEL_WIDTH, dtype=jnp.int32)
    phase = (column_index * 37 % 101).astype(jnp.float32) * (2.0 * math.pi / 101.0)
    return math.sqrt(2.0) * jnp.cos(phase)


def matching_rows(key):
    return jnp.clip(jax.random.normal(jax.random.fold_in(key, 4242), (KEY_VALUE_HEADS, HEAD_WIDTH), jnp.float32), -4.0, 4.0)


def coupling():
    return 0.09 * math.sqrt(MODEL_WIDTH) / MODEL_WIDTH


def draw_hidden_input(key, part):
    random_key, choose_key, level_key = jax.random.split(key, 3)
    pattern = sink_pattern()[None, :]
    sink_rows = jax.random.bernoulli(choose_key, sink_share, (WINDOW_TOKENS, 1))
    random_portion = jnp.clip(jax.random.normal(random_key, (WINDOW_TOKENS, MODEL_WIDTH), jnp.float32), -4.0, 4.0)
    strength = jax.random.uniform(level_key, (WINDOW_TOKENS, 1), jnp.float32, 0.55, 0.9)
    blended = jnp.where(sink_rows, strength * pattern + jnp.sqrt(1.0 - strength * strength) * random_portion, random_portion)
    return jnp.clip(blended, -4.0, 4.0).astype(jnp.bfloat16)


def draw_query_weight(key, part):
    random_portion = jnp.clip(jax.random.normal(jax.random.fold_in(key, 1), (MODEL_WIDTH, QUERY_HEADS * HEAD_WIDTH), jnp.float32), -6.0, 6.0) * MODEL_WIDTH ** (-0.5)
    head_row_list = jnp.repeat(matching_rows(key), QUERY_HEADS // KEY_VALUE_HEADS, axis=0).reshape(QUERY_HEADS * HEAD_WIDTH)
    coherent_part = coupling() * sink_pattern()[:, None] * head_row_list[None, :]
    return (random_portion + coherent_part).astype(jnp.bfloat16)


def draw_key_value_weight(key, part):
    random_portion = jnp.clip(jax.random.normal(jax.random.fold_in(key, 2), (MODEL_WIDTH, 2, KEY_VALUE_HEADS * HEAD_WIDTH), jnp.float32), -6.0, 6.0) * MODEL_WIDTH ** (-0.5)
    head_row_list = matching_rows(key).reshape(KEY_VALUE_HEADS * HEAD_WIDTH)
    coherent_part = coupling() * sink_pattern()[:, None] * head_row_list[None, :]
    key_part = random_portion[:, 0] + coherent_part
    return jnp.stack([key_part, random_portion[:, 1]], axis=1).astype(jnp.bfloat16)


def plant(entries, own_key, smallest, largest):
    longest = entries.shape.index(max(entries.shape))
    spots = []
    for shift in (0, 1):
        where = [jax.random.randint(jax.random.fold_in(own_key, axis), (), 0, length) for axis, length in enumerate(entries.shape)]
        where[longest] = (where[longest] + shift) % entries.shape[longest]
        spots.append(tuple(where))
    return entries.at[spots[0]].set(smallest).at[spots[1]].set(largest)


def shard_levels(stream_key, dims, pieces, smallest, top_value):
    loudness = 1.0
    for dim, blocks in pieces:
        heights = jax.random.uniform(jax.random.fold_in(jax.random.fold_in(stream_key, 6), dim), (blocks,), jnp.float32, smallest / len(pieces), top_value / len(pieces))
        loudness = loudness * jnp.repeat(jnp.exp(heights), dims[dim] // blocks).reshape((-1,) + (1,) * (len(dims) - 1 - dim))
    return loudness


def cumulative_ranks(number_of, slope):
    loads = [(1 << 20) // math.isqrt(grade ** slope) + 1 for grade in range(1, number_of + 1)]
    spread = 1 + sum(loads) // (1 << 30)
    return np.cumsum(np.array([max(1, weight // spread) for weight in loads]))


def ranked_ids(key, dims, count, slope):
    listing = cumulative_ranks(count, slope)
    ticket = jax.random.randint(jax.random.fold_in(key, 1), dims, 0, int(listing[count - 1]))
    rank = jnp.searchsorted(jnp.asarray(listing, jnp.int32), ticket, side="right")
    return jax.random.permutation(jax.random.fold_in(key, 2), count)[rank].astype(jnp.int32)


def split_up(count, total, most, skew):
    weights = [(1 << 20) // math.isqrt(standing ** skew) + 1 for standing in range(2, count + 1)]
    rest, holding = total - most - (count - 1), [1] * (count - 1)
    while rest > 0:
        candidates = [i for i in range(count - 1) if holding[i] < most]
        pool, left = sum([weights[i] for i in candidates]), rest
        for i in candidates:
            more = min(most - holding[i], max(1, left * weights[i] // pool), rest)
            holding[i] = holding[i] + more
            rest = rest - more
    return np.array([most] + holding)


def uneven_parts(key, amount, total, limit, lean):
    if amount == 2:
        one = jax.random.randint(key, (), max(1, total - limit), min(limit, total - 1) + 1)
        return jnp.stack([one, total - one])
    tallies = jnp.asarray(split_up(amount, total, limit, lean), jnp.int32)
    twos = (amount - 1) // 2
    giver, taker = tallies[1:1 + 2 * twos:2], tallies[2:2 + 2 * twos:2]
    slack = jnp.minimum(giver - 1, limit - taker)
    shifted = jax.random.randint(jax.random.fold_in(key, 1), (twos,), 0, 1 << 20) % (slack + 1)
    tallies = tallies.at[1:1 + 2 * twos:2].set(giver - shifted).at[2:2 + 2 * twos:2].set(taker + shifted)
    return tallies[jax.random.permutation(jax.random.fold_in(key, 2), amount)]


def centred(stream_key, shape, scale, limit, cuts=(), kind=jnp.bfloat16):
    values = jax.random.normal(stream_key, shape, jnp.float32) * scale
    if len(cuts) > 0:
        values = shard_levels(stream_key, shape, cuts, -0.22, 0.18) * values
    return jnp.clip(values, min=-limit, max=limit).astype(kind)


def setup_inputs(seed: int = 0, part: int = 0) -> dict:
    splits = jax.random.split(jax.random.key(seed), 14)
    part_splits = jax.random.split(jax.random.fold_in(splits[13], part), 14)
    hidden_input = draw_hidden_input(jax.random.fold_in(jax.random.fold_in(splits[13], part), 71), part)
    norm_gain_vector = jnp.clip(1.0 + 0.18 * jax.random.normal(splits[1], (MODEL_WIDTH,), jnp.float32), 0.099609375, 1.8984375).astype(jnp.bfloat16)
    query_weight = draw_query_weight(jax.random.fold_in(splits[13], 71), part)
    key_value_weight = draw_key_value_weight(jax.random.fold_in(splits[13], 71), part)
    output_weight = centred(splits[4], (QUERY_HEADS * HEAD_WIDTH, MODEL_WIDTH), (QUERY_HEADS * HEAD_WIDTH) ** -0.5, 0.125, ((1, 16),))
    adapter_input_down = centred(splits[5], (ADAPTER_COUNT, MODEL_WIDTH, 3 * ADAPTER_RANK), MODEL_WIDTH ** -0.5, 0.09375, ((0, 16),))
    adapter_query_up = centred(splits[6], (ADAPTER_COUNT, ADAPTER_RANK, QUERY_HEADS * HEAD_WIDTH), ADAPTER_RANK ** -0.5, 0.75, ((0, 16),))
    adapter_key_value_up = centred(splits[7], (ADAPTER_COUNT, 2, ADAPTER_RANK, KEY_VALUE_HEADS * HEAD_WIDTH), ADAPTER_RANK ** -0.5, 0.75, ((0, 16),))
    adapter_output_down = centred(splits[8], (ADAPTER_COUNT, QUERY_HEADS * HEAD_WIDTH, ADAPTER_RANK), (QUERY_HEADS * HEAD_WIDTH) ** -0.5, 0.125, ((0, 16),))
    adapter_output_up = centred(splits[9], (ADAPTER_COUNT, ADAPTER_RANK, MODEL_WIDTH), ADAPTER_RANK ** -0.5, 0.75, ((0, 16),))
    request_lengths = uneven_parts(part_splits[10], REQS, WINDOW_TOKENS, LONGEST, 2).astype(jnp.int32)
    request_adapter = plant(ranked_ids(part_splits[11], (REQS,), ADAPTER_COUNT, 2), jax.random.fold_in(part_splits[11], 3), 0, ADAPTER_COUNT - 1).astype(jnp.int32)
    adapter_table_slot = jax.random.permutation(splits[12], ADAPTER_COUNT).astype(jnp.int32)
    return {"hidden_input": hidden_input, "norm_gain_vector": norm_gain_vector, "query_weight": query_weight, "key_value_weight": key_value_weight, "output_weight": output_weight, "adapter_input_down": adapter_input_down, "adapter_query_up": adapter_query_up, "adapter_key_value_up": adapter_key_value_up, "adapter_output_down": adapter_output_down, "adapter_output_up": adapter_output_up, "request_lengths": request_lengths, "request_adapter": request_adapter, "adapter_table_slot": adapter_table_slot}


epsilon = 1e-05
adapter_scale = 2.0
rope_base = 10000.0
neg_big = -1e+30

def doc_index(positions, doc_ends):
    return lax.optimization_barrier(jnp.sum((doc_ends[None, :] <= positions[:, None]).astype(jnp.int32), axis=1)).astype(jnp.int32)

def rotary_apply(heads, request_offsets):
    half_size = heads.shape[-1] // 2
    frequency = rope_base ** (-jnp.arange(half_size, dtype=jnp.float32) * (2.0 / heads.shape[-1]))
    angles = request_offsets.astype(jnp.float32)[:, None] * frequency[None, :]
    cosine = jnp.cos(angles)[:, None, :]
    sine = jnp.sin(angles)[:, None, :]
    first_half = heads[..., :half_size]
    second_half = heads[..., half_size:]
    return jnp.concatenate([first_half * cosine - second_half * sine, second_half * cosine + first_half * sine], axis=-1)

def allowed_pairs(query_pos, query_doc, key_pos, doc_ends):
    key_doc = doc_index(key_pos, doc_ends)
    distance = query_pos[:, None] - key_pos[None, :]
    return (query_doc[:, None] == key_doc[None, :]) & (distance >= 0) & (distance < WINDOW) & (key_pos[None, :] >= 0)

def reference(hidden_input, norm_gain_vector, query_weight, key_value_weight, output_weight, adapter_input_down, adapter_query_up, adapter_key_value_up, adapter_output_down, adapter_output_up, request_lengths, request_adapter, adapter_table_slot):
    positions = jnp.arange(WINDOW_TOKENS, dtype=jnp.int32)
    doc_ends = jnp.cumsum(request_lengths).astype(jnp.int32)
    doc_ids = doc_index(positions, doc_ends)
    member_mask = doc_ids[:, None] == jnp.arange(REQS, dtype=jnp.int32)[None, :]
    begins = (doc_ends - request_lengths).astype(jnp.int32)
    request_offsets = (positions - lax.optimization_barrier(jnp.sum(jnp.where(member_mask, begins[None, :], 0), axis=1))).astype(jnp.int32)
    widened = hidden_input.astype(jnp.float32)
    normed_hidden = (widened * lax.rsqrt(lax.optimization_barrier(jnp.mean(widened * widened, axis=-1, keepdims=True)) + epsilon) * norm_gain_vector.astype(jnp.float32)).astype(jnp.bfloat16)
    adapter_slot_list = adapter_table_slot[request_adapter]
    down_total = jnp.zeros((WINDOW_TOKENS, 3 * ADAPTER_RANK), jnp.float32)
    for request_number in range(REQS):
        down_product = jnp.dot(normed_hidden, adapter_input_down[adapter_slot_list[request_number]], preferred_element_type=jnp.float32)
        down_total = down_total + jnp.where(member_mask[:, request_number:request_number + 1], down_product, 0.0)
    adapter_down = down_total.astype(jnp.bfloat16)
    query_adapter_delta = jnp.zeros((WINDOW_TOKENS, QUERY_HEADS * HEAD_WIDTH), jnp.float32)
    key_adapter_delta = jnp.zeros((WINDOW_TOKENS, KEY_VALUE_HEADS * HEAD_WIDTH), jnp.float32)
    value_adapter_delta = jnp.zeros((WINDOW_TOKENS, KEY_VALUE_HEADS * HEAD_WIDTH), jnp.float32)
    for request_number in range(REQS):
        input_rows = jnp.where(member_mask[:, request_number:request_number + 1], adapter_down, jnp.zeros_like(adapter_down))
        current_slot = adapter_slot_list[request_number]
        query_adapter_delta = query_adapter_delta + jnp.dot(input_rows[:, :ADAPTER_RANK], adapter_query_up[current_slot], preferred_element_type=jnp.float32)
        key_adapter_delta = key_adapter_delta + jnp.dot(input_rows[:, ADAPTER_RANK:2 * ADAPTER_RANK], adapter_key_value_up[current_slot, 0], preferred_element_type=jnp.float32)
        value_adapter_delta = value_adapter_delta + jnp.dot(input_rows[:, 2 * ADAPTER_RANK:], adapter_key_value_up[current_slot, 1], preferred_element_type=jnp.float32)
    query_complete = jnp.dot(normed_hidden, query_weight, preferred_element_type=jnp.float32) + adapter_scale * query_adapter_delta
    key_value_base = jnp.einsum('td,dck->tck', normed_hidden.astype(jnp.float32), key_value_weight.astype(jnp.float32))
    queries = rotary_apply(query_complete.reshape(WINDOW_TOKENS, QUERY_HEADS, HEAD_WIDTH), request_offsets).astype(jnp.bfloat16)
    key_row_list = rotary_apply((key_value_base[:, 0] + adapter_scale * key_adapter_delta).reshape(WINDOW_TOKENS, KEY_VALUE_HEADS, HEAD_WIDTH), request_offsets).astype(jnp.bfloat16)
    value_row_list = (key_value_base[:, 1] + adapter_scale * value_adapter_delta).reshape(WINDOW_TOKENS, KEY_VALUE_HEADS, HEAD_WIDTH).astype(jnp.bfloat16)
    key_expanded = key_row_list.astype(jnp.float32)
    value_wide = value_row_list.astype(jnp.float32)
    block_length = math.gcd(WINDOW_TOKENS, 512)
    group_width = QUERY_HEADS // KEY_VALUE_HEADS

    def attend(block):
        query_block_rows, block_pos, block_doc = block
        score_matrix = jnp.einsum('xouc,boc->ouxb', query_block_rows.astype(jnp.float32).reshape(block_length, KEY_VALUE_HEADS, group_width, HEAD_WIDTH), key_expanded) * HEAD_WIDTH ** (-0.5)
        allowed = allowed_pairs(block_pos, block_doc, positions, doc_ends)
        score_matrix = jnp.where(allowed, score_matrix, neg_big)
        row_peak = lax.optimization_barrier(jnp.max(score_matrix, axis=-1, keepdims=True))
        weights = jnp.where(allowed, jnp.exp(score_matrix - row_peak), 0.0)
        weight_sum = lax.optimization_barrier(jnp.sum(weights, axis=-1))
        rounded = lax.optimization_barrier(weights.astype(jnp.bfloat16))
        mixed = jnp.einsum('kgts,skd->kgtd', rounded.astype(jnp.float32), value_wide)
        mixed = mixed / weight_sum[..., None]
        return jnp.transpose(mixed, (2, 0, 1, 3)).reshape(block_length, QUERY_HEADS * HEAD_WIDTH).astype(jnp.bfloat16)
    block_count = WINDOW_TOKENS // block_length
    attended_rows = lax.map(attend, (queries.reshape(block_count, block_length, QUERY_HEADS, HEAD_WIDTH), positions.reshape(block_count, block_length), doc_ids.reshape(block_count, block_length)))
    attended_rows = attended_rows.reshape(WINDOW_TOKENS, QUERY_HEADS * HEAD_WIDTH)
    base_output = jnp.dot(attended_rows, output_weight, preferred_element_type=jnp.float32)
    out_sum = jnp.zeros((WINDOW_TOKENS, ADAPTER_RANK), jnp.float32)
    for request_number in range(REQS):
        output_product = jnp.dot(attended_rows, adapter_output_down[adapter_slot_list[request_number]], preferred_element_type=jnp.float32)
        out_sum = out_sum + jnp.where(member_mask[:, request_number:request_number + 1], output_product, 0.0)
    out_down = out_sum.astype(jnp.bfloat16)
    output_adapter_delta = jnp.zeros((WINDOW_TOKENS, MODEL_WIDTH), jnp.float32)
    for request_number in range(REQS):
        input_rows = jnp.where(member_mask[:, request_number:request_number + 1], out_down, jnp.zeros_like(out_down))
        output_adapter_delta = output_adapter_delta + jnp.dot(input_rows, adapter_output_up[adapter_slot_list[request_number]], preferred_element_type=jnp.float32)
    return (base_output + adapter_scale * output_adapter_delta).astype(jnp.bfloat16)
```

```python
import functools
import math

import jax
import jax.numpy as jnp
import numpy as np
from jax import lax
from jax.experimental import pallas as pl
from jax.experimental.pallas import tpu as pltpu
from jax.sharding import Mesh
from jax.sharding import PartitionSpec as P

HEAD_WIDTH = 128
WINDOW = 4096

epsilon = 1e-05
adapter_scale = 2.0
rope_base = 10000.0
masked_score = -1e30
lowest_max = -1e20


def doc_index(positions, doc_ends):
    return jnp.sum((doc_ends[None, :] <= positions[:, None]).astype(jnp.int32), axis=1)


def rotary_apply(heads, cosine, sine):
    half = heads.shape[-1] // 2
    first, second = heads[..., :half], heads[..., half:]
    return jnp.concatenate(
        [first * cosine - second * sine, second * cosine + first * sine], axis=-1
    )


def attention_kernel(
    key_block, chip_rows, heads, slots, kvh, first_kb, full_lo, full_hi, last_kb,
    q_ref, k_ref, v_ref, pos_ref, low_ref, o_ref, q_all, acc, top, mass,
):
    i = pl.program_id(1)
    rows = q_ref.shape[0]
    for h in range(heads):
        q_all[h * rows : (h + 1) * rows, :] = q_ref[:, h * HEAD_WIDTH : (h + 1) * HEAD_WIDTH]
    acc[...] = jnp.zeros_like(acc)
    top[...] = jnp.full_like(top, lowest_max)
    mass[...] = jnp.zeros_like(mass)
    factor = math.log2(math.e) * HEAD_WIDTH ** (-0.5)
    per_chip = chip_rows // key_block

    def step(kb, masked):
        start = slots[kb // per_chip] * chip_rows + (kb % per_chip) * key_block
        start = pl.multiple_of(start, key_block)
        keys = k_ref[pl.ds(start, key_block), :]
        scores = lax.dot_general(
            keys, q_all[...], (((1,), (1,)), ((), ())), preferred_element_type=jnp.float32
        )
        if masked:
            key_pos = kb * key_block + lax.broadcasted_iota(jnp.int32, (key_block, rows), 0)
            allowed = (key_pos >= low_ref[...]) & (key_pos <= pos_ref[...])
            scores = jnp.concatenate(
                [
                    jnp.where(allowed, scores[:, h * rows : (h + 1) * rows], masked_score)
                    for h in range(heads)
                ],
                axis=1,
            )
        old = top[...]
        new = jnp.maximum(old, jnp.max(scores, axis=0, keepdims=True))
        weights = jnp.exp2((scores - new) * factor)
        shrink = jnp.exp2((old - new) * factor)
        top[...] = new
        mass[...] = mass[...] * shrink + jnp.sum(weights, axis=0, keepdims=True)
        values = v_ref[:, pl.ds(start, key_block)]
        acc[...] = acc[...] * shrink + jnp.dot(
            values, weights.astype(jnp.bfloat16), preferred_element_type=jnp.float32
        )

    def masked_step(kb, carry):
        step(kb, True)
        return carry

    def full_step(kb, carry):
        step(kb, False)
        return carry

    lax.fori_loop(first_kb[i], full_lo[i], masked_step, 0)
    lax.fori_loop(full_lo[i], full_hi[i], full_step, 0)
    lax.fori_loop(full_hi[i], last_kb[i] + 1, masked_step, 0)
    mixed = acc[...] / mass[...]
    for h in range(heads):
        part = mixed[:, h * rows : (h + 1) * rows]
        o_ref[:, h * HEAD_WIDTH : (h + 1) * HEAD_WIDTH] = part.T.astype(o_ref.dtype)


def attention(queries, keys, values, positions, lows, slots, kvh, chip_rows):
    tokens, query_cols = queries.shape
    kv_heads = keys.shape[1] // HEAD_WIDTH
    heads = query_cols // HEAD_WIDTH // kv_heads
    total = keys.shape[0]
    q_block = math.gcd(tokens, 256)
    key_block = math.gcd(chip_rows, 512)
    blocks = tokens // q_block
    block_pos = positions.reshape(blocks, q_block)
    block_low = lows.reshape(blocks, q_block)
    first_kb = block_low[:, 0] // key_block
    last_kb = block_pos[:, -1] // key_block
    full_hi = block_pos[:, 0] // key_block
    full_lo = jnp.minimum((block_low[:, -1] + key_block - 1) // key_block, full_hi)
    full_lo = jnp.maximum(full_lo, first_kb)
    group = heads * HEAD_WIDTH
    return pl.pallas_call(
        functools.partial(attention_kernel, key_block, chip_rows, heads),
        out_shape=jax.ShapeDtypeStruct((tokens, query_cols), jnp.bfloat16),
        grid_spec=pltpu.PrefetchScalarGridSpec(
            num_scalar_prefetch=6,
            grid=(kv_heads, blocks),
            in_specs=[
                pl.BlockSpec((q_block, group), lambda j, i, *s: (i, j)),
                pl.BlockSpec((total, HEAD_WIDTH), lambda j, i, sl, kvh, *s: (0, kvh[j])),
                pl.BlockSpec((HEAD_WIDTH, total), lambda j, i, sl, kvh, *s: (kvh[j], 0)),
                pl.BlockSpec((1, q_block), lambda j, i, *s: (0, i)),
                pl.BlockSpec((1, q_block), lambda j, i, *s: (0, i)),
            ],
            out_specs=pl.BlockSpec((q_block, group), lambda j, i, sl, kvh, *s: (i, kvh[j])),
            scratch_shapes=[
                pltpu.VMEM((heads * q_block, HEAD_WIDTH), jnp.bfloat16),
                pltpu.VMEM((HEAD_WIDTH, heads * q_block), jnp.float32),
                pltpu.VMEM((1, heads * q_block), jnp.float32),
                pltpu.VMEM((1, heads * q_block), jnp.float32),
            ],
        ),
        compiler_params=pltpu.CompilerParams(vmem_limit_bytes=56 * 1024 * 1024),
        name="window_attention",
    )(
        slots, kvh, first_kb, full_lo, full_hi, last_kb,
        queries, keys, values, positions[None, :], lows[None, :],
    )


class Ring:
    def __init__(self, order):
        self.order = order
        self.count = len(order)
        place = np.zeros(self.count, np.int32)
        place[np.array(order)] = np.arange(self.count)
        here = jnp.asarray(place)[lax.axis_index("chip")]
        ahead = self.count // 2
        behind = (self.count - 1) // 2
        self.steps = [(True, k) for k in range(1, ahead + 1)]
        self.steps += [(False, k) for k in range(1, behind + 1)]
        self.steps.sort(key=lambda s: s[1])
        offsets = [0] + [k if forward else -k for forward, k in self.steps]
        table = np.zeros((self.count, self.count), np.int32)
        back = np.zeros((self.count, self.count), np.int32)
        for r in range(self.count):
            for n, offset in enumerate(offsets):
                table[r, n] = order[(r - offset) % self.count]
                back[r, table[r, n]] = n
        self.source = jnp.asarray(table)[here]
        self.slot = jnp.asarray(back)[here]
        pairs = [(order[r], order[(r + 1) % self.count]) for r in range(self.count)]
        self.pairs = {True: pairs, False: [(b, a) for a, b in pairs]}

    def gather(self, shard):
        pieces, latest = [shard], {True: shard, False: shard}
        for forward, _ in self.steps:
            latest[forward] = lax.ppermute(latest[forward], "chip", self.pairs[forward])
            pieces.append(latest[forward])
        return pieces


def halves(first, mine, other, axis):
    return jnp.where(
        first,
        jnp.concatenate([mine, other], axis=axis),
        jnp.concatenate([other, mine], axis=axis),
    )


def shards(
    planes, cores, ring_order,
    hidden_input, norm_gain_vector, query_weight, key_value_weight, output_weight,
    adapter_input_down, adapter_query_up, adapter_key_value_up, adapter_output_down,
    adapter_output_up, request_lengths, request_adapter, adapter_table_slot,
):
    swap = [(0, 1), (1, 0)]
    core = lax.axis_index("core")
    chip = lax.axis_index("chip")
    first_core = core == 0
    ring = Ring(ring_order)
    chips = ring.count

    def other_core(x):
        return lax.ppermute(x, "core", swap)

    table_slots = adapter_table_slot[request_adapter]
    requests = request_adapter.shape[0]
    local_total = adapter_input_down.shape[0]
    me = chip * cores + core
    mine = (table_slots // local_total) == me
    local_position = table_slots % local_total

    def chosen(table):
        picked = [
            jnp.where(mine[r], table[local_position[r]], jnp.zeros_like(table[0]))
            for r in range(requests)
        ]
        return picked

    axes = ("chip", "core")
    downs, up_query, up_kv = lax.psum(
        (chosen(adapter_input_down), chosen(adapter_query_up), chosen(adapter_key_value_up)), axes
    )

    query_weight_rows = query_weight
    kv_rows_weight = key_value_weight.reshape(key_value_weight.shape[0], -1)
    kv_cols = key_value_weight.shape[2] // cores
    query_cols = query_weight.shape[1] // cores
    if cores == 2:

        def exchange(w, width):
            keep = lax.dynamic_slice_in_dim(w, core * width, width, axis=w.ndim - 1)
            give = lax.dynamic_slice_in_dim(w, (1 - core) * width, width, axis=w.ndim - 1)
            return halves(first_core, keep, other_core(give), 0)

        query_weight_rows = exchange(query_weight, query_cols)
        kv_rows_weight = exchange(key_value_weight, kv_cols)
        kv_rows_weight = kv_rows_weight.reshape(kv_rows_weight.shape[0], -1)
    weight_rows = query_weight_rows.shape[0]
    half_cols = query_cols // 2
    plane = lax.axis_index("groups") % 2
    own_query = lax.dynamic_slice_in_dim(query_weight_rows, plane * half_cols, half_cols, axis=1)
    rest_query = lax.dynamic_slice_in_dim(
        query_weight_rows, (1 - plane) * half_cols, half_cols, axis=1
    )
    kv_pieces = ring.gather(kv_rows_weight)
    own_pieces = ring.gather(own_query)
    across = [(g, g ^ 1) for g in range(planes)]
    rest_pieces = [rest_query] + [lax.ppermute(p, "groups", across) for p in own_pieces[1:]]
    out_pieces = ring.gather(output_weight)

    rows = hidden_input.shape[0]
    tokens = rows * cores
    positions = chip * tokens + jnp.arange(tokens, dtype=jnp.int32)
    doc_ends = jnp.cumsum(request_lengths)
    begins = doc_ends - request_lengths
    doc_ids = doc_index(positions, doc_ends)
    member = doc_ids[:, None] == jnp.arange(requests, dtype=jnp.int32)[None, :]
    starts = jnp.sum(jnp.where(member, begins[None, :], 0), axis=1)
    offsets = positions - starts
    lows = jnp.maximum(starts, positions - (WINDOW - 1))

    widened = hidden_input.astype(jnp.float32)
    normed_mine = (
        widened
        * lax.rsqrt(jnp.mean(widened * widened, axis=-1, keepdims=True) + epsilon)
        * norm_gain_vector.astype(jnp.float32)
    ).astype(jnp.bfloat16)
    normed = normed_mine
    my_member = member
    if cores == 2:
        normed = halves(first_core, normed_mine, other_core(normed_mine), 0)
        my_member = lax.dynamic_slice_in_dim(member, core * rows, rows, axis=0)

    def dot(a, b):
        return jnp.dot(a, b, preferred_element_type=jnp.float32)

    kv_base = own_base = rest_base = 0.0
    for n in range(chips):
        block = lax.dynamic_slice_in_dim(normed, ring.source[n] * weight_rows, weight_rows, axis=1)
        kv_base = kv_base + dot(block, kv_pieces[n])
        own_base = own_base + dot(block, own_pieces[n])
        rest_base = rest_base + dot(block, rest_pieces[n])

    rank = adapter_input_down.shape[2] // 3
    down_total = jnp.zeros((rows, 3 * rank), jnp.float32)
    for r in range(requests):
        down_total = down_total + jnp.where(my_member[:, r : r + 1], dot(normed_mine, downs[r]), 0.0)
    down_rows = down_total.astype(jnp.bfloat16)
    if cores == 2:
        down_rows = halves(first_core, down_rows, other_core(down_rows), 0)

    def spread(part):
        return jnp.concatenate(
            [jnp.where(member[:, r : r + 1], part, jnp.zeros_like(part)) for r in range(requests)],
            axis=1,
        )

    def columns(ups, at, width):
        return jnp.concatenate(
            [lax.dynamic_slice_in_dim(u, at, width, axis=1) for u in ups], axis=0
        )

    query_start = core * query_cols
    spread_query = spread(down_rows[:, :rank])
    own_delta = dot(
        spread_query, columns(up_query, query_start + plane * half_cols, half_cols)
    )
    rest_delta = dot(
        spread_query, columns(up_query, query_start + (1 - plane) * half_cols, half_cols)
    )
    kv_start = core * kv_cols
    key_delta = dot(
        spread(down_rows[:, rank : 2 * rank]), columns([u[0] for u in up_kv], kv_start, kv_cols)
    )
    value_delta = dot(
        spread(down_rows[:, 2 * rank :]), columns([u[1] for u in up_kv], kv_start, kv_cols)
    )

    half = HEAD_WIDTH // 2
    frequency = rope_base ** (-jnp.arange(half, dtype=jnp.float32) * (2.0 / HEAD_WIDTH))
    angles = offsets.astype(jnp.float32)[:, None] * frequency[None, :]
    cosine, sine = jnp.cos(angles)[:, None, :], jnp.sin(angles)[:, None, :]

    def rotated(full):
        heads = full.reshape(tokens, -1, HEAD_WIDTH)
        return rotary_apply(heads, cosine, sine).astype(jnp.bfloat16).reshape(tokens, -1)

    keys = rotated(kv_base[:, :kv_cols] + adapter_scale * key_delta)
    values = (kv_base[:, kv_cols:] + adapter_scale * value_delta).astype(jnp.bfloat16).T
    key_all = jnp.concatenate(ring.gather(keys), axis=0)
    value_all = jnp.concatenate(ring.gather(values), axis=1)
    queries = jnp.concatenate(
        [rotated(own_base + adapter_scale * own_delta), rotated(rest_base + adapter_scale * rest_delta)],
        axis=1,
    )
    kv_heads = kv_cols // HEAD_WIDTH
    split = kv_heads // 2
    index = jnp.arange(kv_heads, dtype=jnp.int32)
    kvh = (index + plane * split) % kv_heads
    attended = attention(queries, key_all, value_all, positions, lows, ring.slot, kvh, tokens)

    out_downs, out_ups = lax.psum(
        (chosen(adapter_output_down), chosen(adapter_output_up)), axes
    )
    out_weight = jnp.take(jnp.stack(out_pieces), ring.slot, axis=0)
    if cores == 2:
        attended = halves(first_core, attended, other_core(attended), 1)
    my_attended = attended
    if cores == 2:
        my_attended = lax.dynamic_slice_in_dim(attended, core * rows, rows, axis=0)
    out_total = jnp.zeros((rows, rank), jnp.float32)
    for r in range(requests):
        out_total = out_total + jnp.where(my_member[:, r : r + 1], dot(my_attended, out_downs[r]), 0.0)
    out_down = out_total.astype(jnp.bfloat16)
    piece_cols = output_weight.shape[1]
    ups = jnp.concatenate(out_ups, axis=0)
    if cores == 2:
        out_down = halves(first_core, out_down, other_core(out_down), 0)
        out_weight = jnp.transpose(out_weight, (1, 0, 2)).reshape(output_weight.shape[0], -1)
        ups = ups.reshape(ups.shape[0], chips, cores, piece_cols)
        ups = lax.dynamic_index_in_dim(ups, core, axis=2, keepdims=False)
        ups = ups.reshape(ups.shape[0], chips * piece_cols)
        result = dot(attended, out_weight) + adapter_scale * dot(spread(out_down), ups)
        result = result.astype(jnp.bfloat16)
        keep = lax.dynamic_slice_in_dim(result, core * rows, rows, axis=0)
        give = lax.dynamic_slice_in_dim(result, (1 - core) * rows, rows, axis=0)
        keep = keep.reshape(rows, chips, 1, piece_cols)
        got = other_core(give).reshape(rows, chips, 1, piece_cols)
        return halves(first_core, keep, got, 2).reshape(rows, -1)
    out_down = lax.psum(out_down, "sub")
    out_weight = jnp.transpose(out_weight, (1, 0, 2)).reshape(output_weight.shape[0], -1)
    partial_out = dot(attended, out_weight).astype(jnp.bfloat16)
    summed = lax.psum_scatter(partial_out, "sub", scatter_dimension=1, tiled=True)
    delta = dot(spread(out_down), ups)
    return (summed.astype(jnp.float32) + adapter_scale * delta).astype(jnp.bfloat16)


def solution(mesh):
    planes, seq, sub = mesh.devices.shape
    cores = 2 if sub == 1 else 1
    chips = seq // cores
    if cores == 2:
        order = list(range(0, chips, 2)) + list(range(chips - 1, 0, -2))
    else:
        order = list(range(chips))
    split = Mesh(
        mesh.devices.reshape(planes, chips, cores, sub), ("groups", "chip", "core", "sub")
    )
    seq_axes = ("chip", "core")
    return jax.shard_map(
        functools.partial(shards, planes, cores, order),
        mesh=split,
        in_specs=(
            P(("groups", "chip", "core"), None),
            P(),
            P(seq_axes, "sub"),
            P(seq_axes, None, "sub"),
            P("sub", seq_axes),
            P(seq_axes, None, None),
            P(seq_axes, None, "sub"),
            P(seq_axes, None, None, "sub"),
            P(seq_axes, "sub", None),
            P(seq_axes, None, "sub"),
            P("groups"),
            P("groups"),
            P(),
        ),
        out_specs=P(("groups", "chip", "core"), "sub"),
        check_vma=False,
    )
```

```python
import functools
import math

import jax
import jax.numpy as jnp
import numpy as np
from jax import lax
from jax.experimental import pallas as pl
from jax.experimental.pallas import tpu as pltpu
from jax.sharding import Mesh
from jax.sharding import PartitionSpec as P

HEAD_WIDTH = 128
WINDOW = 4096

epsilon = 1e-05
adapter_scale = 2.0
rope_base = 10000.0
masked_score = -1e30
lowest_max = -1e20


def doc_index(positions, doc_ends):
    return jnp.sum((doc_ends[None, :] <= positions[:, None]).astype(jnp.int32), axis=1)


def attention_kernel(
    key_block, chip_rows, heads, slots, kvh, first_kb, full_lo, full_hi, last_kb,
    q_ref, k_ref, v_ref, pos_ref, low_ref, o_ref, q_all, acc, top, mass,
):
    i = pl.program_id(1)
    rows = q_ref.shape[0]
    for h in range(heads):
        q_all[h * rows : (h + 1) * rows, :] = q_ref[:, h * HEAD_WIDTH : (h + 1) * HEAD_WIDTH]
    acc[...] = jnp.zeros_like(acc)
    top[...] = jnp.full_like(top, lowest_max)
    mass[...] = jnp.zeros_like(mass)
    factor = math.log2(math.e) * HEAD_WIDTH ** (-0.5)
    per_chip = chip_rows // key_block

    def step(kb, masked):
        start = slots[kb // per_chip] * chip_rows + (kb % per_chip) * key_block
        start = pl.multiple_of(start, key_block)
        keys = k_ref[pl.ds(start, key_block), :]
        scores = lax.dot_general(
            keys, q_all[...], (((1,), (1,)), ((), ())), preferred_element_type=jnp.float32
        )
        if masked:
            key_pos = kb * key_block + lax.broadcasted_iota(jnp.int32, (key_block, rows), 0)
            allowed = (key_pos >= low_ref[...]) & (key_pos <= pos_ref[...])
            scores = jnp.concatenate(
                [
                    jnp.where(allowed, scores[:, h * rows : (h + 1) * rows], masked_score)
                    for h in range(heads)
                ],
                axis=1,
            )
        old = top[...]
        new = jnp.maximum(old, jnp.max(scores, axis=0, keepdims=True))
        weights = jnp.exp2((scores - new) * factor)
        shrink = jnp.exp2((old - new) * factor)
        top[...] = new
        mass[...] = mass[...] * shrink + jnp.sum(weights, axis=0, keepdims=True)
        values = v_ref[:, pl.ds(start, key_block)]
        acc[...] = acc[...] * shrink + jnp.dot(
            values, weights.astype(jnp.bfloat16), preferred_element_type=jnp.float32
        )

    def masked_step(kb, carry):
        step(kb, True)
        return carry

    def full_step(kb, carry):
        step(kb, False)
        return carry

    lax.fori_loop(first_kb[i], full_lo[i], masked_step, 0)
    lax.fori_loop(full_lo[i], full_hi[i], full_step, 0)
    lax.fori_loop(full_hi[i], last_kb[i] + 1, masked_step, 0)
    mixed = acc[...] / mass[...]
    for h in range(heads):
        part = mixed[:, h * rows : (h + 1) * rows]
        o_ref[:, h * HEAD_WIDTH : (h + 1) * HEAD_WIDTH] = part.T.astype(o_ref.dtype)


def attention(queries, keys, values, positions, lows, slots, kvh, chip_rows):
    tokens, query_cols = queries.shape
    kv_heads = keys.shape[1] // HEAD_WIDTH
    heads = query_cols // HEAD_WIDTH // kv_heads
    total = keys.shape[0]
    q_block = math.gcd(tokens, 256)
    key_block = math.gcd(chip_rows, 512)
    blocks = tokens // q_block
    block_pos = positions.reshape(blocks, q_block)
    block_low = lows.reshape(blocks, q_block)
    first_kb = block_low[:, 0] // key_block
    last_kb = block_pos[:, -1] // key_block
    full_hi = block_pos[:, 0] // key_block
    full_lo = jnp.minimum((block_low[:, -1] + key_block - 1) // key_block, full_hi)
    full_lo = jnp.maximum(full_lo, first_kb)
    group = heads * HEAD_WIDTH
    return pl.pallas_call(
        functools.partial(attention_kernel, key_block, chip_rows, heads),
        out_shape=jax.ShapeDtypeStruct((tokens, query_cols), jnp.bfloat16),
        grid_spec=pltpu.PrefetchScalarGridSpec(
            num_scalar_prefetch=6,
            grid=(kv_heads, blocks),
            in_specs=[
                pl.BlockSpec((q_block, group), lambda j, i, *s: (i, j)),
                pl.BlockSpec((total, HEAD_WIDTH), lambda j, i, *s: (0, j)),
                pl.BlockSpec((HEAD_WIDTH, total), lambda j, i, *s: (j, 0)),
                pl.BlockSpec((1, q_block), lambda j, i, *s: (0, i)),
                pl.BlockSpec((1, q_block), lambda j, i, *s: (0, i)),
            ],
            out_specs=pl.BlockSpec((q_block, group), lambda j, i, sl, kvh, *s: (i, kvh[j])),
            scratch_shapes=[
                pltpu.VMEM((heads * q_block, HEAD_WIDTH), jnp.bfloat16),
                pltpu.VMEM((HEAD_WIDTH, heads * q_block), jnp.float32),
                pltpu.VMEM((1, heads * q_block), jnp.float32),
                pltpu.VMEM((1, heads * q_block), jnp.float32),
            ],
        ),
        compiler_params=pltpu.CompilerParams(vmem_limit_bytes=56 * 1024 * 1024),
        name="window_attention",
    )(
        slots, kvh, first_kb, full_lo, full_hi, last_kb,
        queries, keys, values, positions[None, :], lows[None, :],
    )


class Ring:
    def __init__(self, order):
        self.order = order
        self.count = len(order)
        place = np.zeros(self.count, np.int32)
        place[np.array(order)] = np.arange(self.count)
        here = jnp.asarray(place)[lax.axis_index("chip")]
        self.here = here
        ahead = self.count // 2
        behind = (self.count - 1) // 2
        self.steps = [(True, k) for k in range(1, ahead + 1)]
        self.steps += [(False, k) for k in range(1, behind + 1)]
        self.steps.sort(key=lambda s: s[1])
        offsets = [0] + [k if forward else -k for forward, k in self.steps]
        table = np.zeros((self.count, self.count), np.int32)
        back = np.zeros((self.count, self.count), np.int32)
        for r in range(self.count):
            for n, offset in enumerate(offsets):
                table[r, n] = order[(r - offset) % self.count]
                back[r, table[r, n]] = n
        self.source = jnp.asarray(table)[here]
        self.slot = jnp.asarray(back)[here]
        pairs = [(order[r], order[(r + 1) % self.count]) for r in range(self.count)]
        self.pairs = {True: pairs, False: [(b, a) for a, b in pairs]}

    def gather(self, shard):
        pieces, latest = [shard], {True: shard, False: shard}
        for forward, _ in self.steps:
            latest[forward] = lax.ppermute(latest[forward], "chip", self.pairs[forward])
            pieces.append(latest[forward])
        return pieces

    def total(self, parts):
        ahead = max(k for forward, k in self.steps if forward)
        behind = self.count - 1 - ahead

        def part(k):
            return lax.dynamic_index_in_dim(parts, self.after(k), 0, keepdims=False)

        sums = {True: part(ahead), False: part(-behind)}
        for k in range(ahead - 1, -1, -1):
            for forward in (True, False):
                if not forward and k >= behind:
                    continue
                sums[forward] = lax.ppermute(sums[forward], "chip", self.pairs[forward])
                if k > 0:
                    sums[forward] = sums[forward] + part(k if forward else -k)
        return sums[True] + sums[False] + part(0)

    def after(self, k):
        order = jnp.asarray(np.array(self.order, np.int32))
        return order[(self.here + k) % self.count]

    def everywhere(self, rows):
        count, width = rows.shape
        part = self.total(rows.reshape(self.count, count // self.count, width))
        parts = jnp.stack(self.gather(part))
        return jnp.take(parts, self.slot, axis=0).reshape(count, width)


def halves(first, mine, other, axis):
    return jnp.where(
        first,
        jnp.concatenate([mine, other], axis=axis),
        jnp.concatenate([other, mine], axis=axis),
    )


def assemble_kernel(slots, core, keep_ref, got_ref, o_ref):
    width = keep_ref.shape[1]

    @pl.when(core[0] == 0)
    def _():
        o_ref[:, :width] = keep_ref[...]
        o_ref[:, width:] = got_ref[...]

    @pl.when(core[0] != 0)
    def _():
        o_ref[:, :width] = got_ref[...]
        o_ref[:, width:] = keep_ref[...]


def assemble(keep, got, slots, core, chips):
    rows, cols = keep.shape
    width = cols // chips
    block = pl.BlockSpec((rows, width), lambda j, slots, core: (0, slots[j]))
    return pl.pallas_call(
        assemble_kernel,
        out_shape=jax.ShapeDtypeStruct((rows, 2 * cols), keep.dtype),
        grid_spec=pltpu.PrefetchScalarGridSpec(
            num_scalar_prefetch=2,
            grid=(chips,),
            in_specs=[block, block],
            out_specs=pl.BlockSpec((rows, 2 * width), lambda j, slots, core: (0, j)),
        ),
        name="assemble_output",
    )(slots, core[None], keep, got)


def shards(
    planes, cores, ring_order,
    hidden_input, norm_gain_vector, query_weight, key_value_weight, output_weight,
    adapter_input_down, adapter_query_up, adapter_key_value_up, adapter_output_down,
    adapter_output_up, request_lengths, request_adapter, adapter_table_slot,
):
    core = lax.axis_index("core").astype(jnp.int32)
    chip = lax.axis_index("chip").astype(jnp.int32)
    first_core = core == 0
    ring = Ring(ring_order)
    chips = ring.count
    plane = (lax.axis_index("groups") % 2).astype(jnp.int32)
    across = [(g, g ^ 1) for g in range(planes)]

    def other_core(x):
        return lax.ppermute(x, "core", [(0, 1), (1, 0)])

    def other_plane(x):
        return lax.ppermute(x, "groups", across)

    def cut(x, at, width, axis):
        return lax.dynamic_slice_in_dim(x, at, width, axis=axis)

    def dot(a, b):
        return jnp.dot(a, b, preferred_element_type=jnp.float32)

    def dot_rows(a, b):
        return lax.dot_general(a, b, (((1,), (1,)), ((), ())), preferred_element_type=jnp.float32)

    rows = hidden_input.shape[0]
    tokens = rows * cores
    query_cols = query_weight.shape[1] // cores
    kv_cols = key_value_weight.shape[2] // cores

    def grouped(of):
        pieces = []
        for side in range(2):
            half_q, half_kv = query_cols // 2, kv_cols // 2
            pieces.append(
                jnp.concatenate(
                    [
                        cut(query_weight, of * query_cols + side * half_q, half_q, 1),
                        cut(key_value_weight[:, 0], of * kv_cols + side * half_kv, half_kv, 1),
                        cut(key_value_weight[:, 1], of * kv_cols + side * half_kv, half_kv, 1),
                    ],
                    axis=1,
                )
            )
        return jnp.stack(pieces)

    weight = grouped(core)
    if cores == 2:
        weight = halves(first_core, weight, other_core(grouped(1 - core)), 1)
    weight_rows = weight.shape[1]
    own_weight = lax.dynamic_index_in_dim(weight, plane, 0, keepdims=False)
    rest_weight = lax.dynamic_index_in_dim(weight, 1 - plane, 0, keepdims=False)
    own_pieces = ring.gather(own_weight)
    rest_pieces = [rest_weight] + [other_plane(p) for p in own_pieces[1:]]

    widened = hidden_input.astype(jnp.float32)
    normed_mine = (
        widened
        * lax.rsqrt(jnp.mean(widened * widened, axis=-1, keepdims=True) + epsilon)
        * norm_gain_vector.astype(jnp.float32)
    ).astype(jnp.bfloat16)
    normed = normed_mine
    if cores == 2:
        normed = halves(first_core, normed_mine, other_core(normed_mine), 0)

    table_slots = adapter_table_slot[request_adapter]
    requests = request_adapter.shape[0]
    per_core = requests // cores
    local_total = adapter_input_down.shape[0]
    mine = (table_slots // local_total) == chip * cores + core
    local_position = table_slots % local_total
    rank = adapter_input_down.shape[2] // 3

    def picked(table, r):
        entry = lax.dynamic_index_in_dim(table, local_position[r], 0, keepdims=False)
        return jnp.where(mine[r], entry, jnp.zeros_like(entry))

    def in_rows(of):
        chosen = [
            jnp.swapaxes(picked(adapter_input_down, of * per_core + i), 0, 1)
            for i in range(per_core)
        ]
        down = [c[part * rank : (part + 1) * rank] for part in range(3) for c in chosen]
        ups = []
        for r in range(requests):
            kv = picked(adapter_key_value_up, r)
            ups.append(
                jnp.concatenate(
                    [
                        cut(picked(adapter_query_up, r), of * query_cols, query_cols, 1),
                        cut(kv[0], of * kv_cols, kv_cols, 1),
                        cut(kv[1], of * kv_cols, kv_cols, 1),
                    ],
                    axis=1,
                )
            )
        width = adapter_input_down.shape[1]
        return jnp.concatenate(down + [jnp.concatenate(ups, axis=0).reshape(-1, width)], axis=0)

    piece_cols = output_weight.shape[1]
    out_cols = adapter_output_up.shape[2] // cores

    def out_rows(of):
        ups = []
        for r in range(requests):
            up = picked(adapter_output_up, r).reshape(rank, chips, cores, -1)
            up = lax.dynamic_index_in_dim(up, of, 2, keepdims=False)
            ups.append(up.reshape(rank, out_cols))
        down = [
            jnp.swapaxes(picked(adapter_output_down, of * per_core + i), 0, 1).reshape(-1, out_cols)
            for i in range(per_core)
        ]
        return jnp.concatenate(ups + down, axis=0)

    def both_cores(make):
        if cores == 1:
            return make(core)
        return make(core) + other_core(make(1 - core))

    in_table = ring.everywhere(both_cores(in_rows))
    down_table = in_table[: 3 * per_core * rank]
    up_table = in_table[3 * per_core * rank :].reshape(requests * rank, query_cols + 2 * kv_cols)

    half_rows = output_weight.shape[0] // 2
    out_table, out_weight, _ = lax.optimization_barrier(
        (both_cores(out_rows), output_weight, own_pieces[-1])
    )
    out_own = ring.gather(cut(out_weight, plane * half_rows, half_rows, 0))
    out_rest = [cut(out_weight, (1 - plane) * half_rows, half_rows, 0)]
    out_rest += [other_plane(p) for p in out_own[1:]]
    out_table = ring.everywhere(out_table)

    positions = chip * tokens + jnp.arange(tokens, dtype=jnp.int32)
    doc_ends = jnp.cumsum(request_lengths)
    begins = doc_ends - request_lengths
    doc_ids = doc_index(positions, doc_ends)
    member = doc_ids[:, None] == jnp.arange(requests, dtype=jnp.int32)[None, :]
    starts = jnp.sum(jnp.where(member, begins[None, :], 0), axis=1)
    offsets = positions - starts
    lows = jnp.maximum(starts, positions - (WINDOW - 1))

    own_base = rest_base = 0.0
    for n in range(chips):
        block = cut(normed, ring.source[n] * weight_rows, weight_rows, 1)
        own_base = own_base + dot(block, own_pieces[n])
        rest_base = rest_base + dot(block, rest_pieces[n])

    request_of = core * per_core + jnp.arange(per_core * rank, dtype=jnp.int32) // rank
    my_columns = doc_ids[:, None] == request_of[None, :]
    my_columns = jnp.concatenate([my_columns] * 3, axis=1)
    down_rows = dot_rows(normed, down_table).astype(jnp.bfloat16)
    down_rows = jnp.where(my_columns, down_rows, jnp.zeros_like(down_rows))
    width = per_core * rank
    parts = [down_rows[:, p * width : (p + 1) * width] for p in range(3)]
    if cores == 2:
        got = other_core(down_rows)
        parts = [
            halves(first_core, parts[p], got[:, p * width : (p + 1) * width], 1) for p in range(3)
        ]

    half_q, half_kv = query_cols // 2, kv_cols // 2

    def full(base, side):
        places = [
            (0, half_q, side * half_q),
            (half_q, half_kv, query_cols + side * half_kv),
            (half_q + half_kv, half_kv, query_cols + kv_cols + side * half_kv),
        ]
        return [
            base[:, at : at + size] + adapter_scale * dot(parts[n], cut(up_table, start, size, 1))
            for n, (at, size, start) in enumerate(places)
        ]

    own_full, rest_full = full(own_base, plane), full(rest_base, 1 - plane)

    half = HEAD_WIDTH // 2
    frequency = rope_base ** (-jnp.arange(half, dtype=jnp.float32) * (2.0 / HEAD_WIDTH))
    angles = offsets.astype(jnp.float32)[:, None] * frequency[None, :]
    cosine, sine = jnp.cos(angles), jnp.sin(angles)
    cosine = jnp.concatenate([cosine, cosine], axis=1)
    sine = jnp.concatenate([-sine, sine], axis=1)

    def rotated(*sides):
        heads = [
            side[:, h : h + HEAD_WIDTH] for side in sides for h in range(0, side.shape[1], HEAD_WIDTH)
        ]
        turned = [x * cosine + jnp.roll(x, half, axis=1) * sine for x in heads]
        return jnp.concatenate([x.astype(jnp.bfloat16) for x in turned], axis=1)

    keys = rotated(own_full[1], rest_full[1])
    values = jnp.concatenate([own_full[2], rest_full[2]], axis=1).astype(jnp.bfloat16).T
    queries = rotated(own_full[0], rest_full[0])

    reach = -(-(WINDOW - 1) // tokens)
    if cores == 2:
        stride, hops = 2, -(-reach // 2)
    else:
        stride, hops = 1, reach
    hops = min(hops, (chips - 1) // stride)
    up = [(q, q + stride) for q in range(chips - stride)]

    def earlier(x):
        pieces = [x]
        for _ in range(hops):
            pieces.append(lax.ppermute(pieces[-1], "chip", up))
        if stride == 2:
            to_odd = [(q, q + 1) for q in range(0, chips, 2)]
            to_even = [(q + 1, q) for q in range(0, chips, 2)]
            for n in range(hops + 1):
                pairs = to_odd if n == 0 else to_even if n == hops else to_odd + to_even
                pieces.append(lax.ppermute(pieces[n], "chip", pairs))
        return pieces

    origin = [chip - stride * n for n in range(hops + 1)]
    if stride == 2:
        origin += [(chip ^ 1) - stride * n for n in range(hops + 1)]
    origin = jnp.stack(origin)
    key_slots = jnp.argmax(
        origin[None, :] == jnp.arange(chips, dtype=jnp.int32)[:, None], axis=1
    ).astype(jnp.int32)
    key_all = jnp.concatenate(earlier(keys), axis=0)
    value_all = jnp.concatenate(earlier(values), axis=1)

    kv_heads = kv_cols // HEAD_WIDTH
    place = (jnp.arange(kv_heads, dtype=jnp.int32) + plane * (kv_heads // 2)) % kv_heads
    attended = attention(queries, key_all, value_all, positions, lows, key_slots, place, tokens)

    ups = out_table[: requests * rank]
    downs = out_table[requests * rank :].reshape(per_core * rank, -1)
    every_request = jnp.arange(requests * rank, dtype=jnp.int32) // rank
    columns = doc_ids[:, None] == every_request[None, :]
    if cores == 2:
        downs = halves(first_core, downs, other_core(downs), 0)
        ups = jnp.take(ups.reshape(-1, chips, piece_cols), ring.source, axis=1)
        ups = ups.reshape(requests * rank, out_cols)
        own_out = jnp.concatenate(out_own, axis=1)
        rest_out = jnp.concatenate(out_rest, axis=1)
        own_down = cut(downs, plane * half_rows, half_rows, 1)
        rest_down = cut(downs, (1 - plane) * half_rows, half_rows, 1)
        got = other_core(attended)
        here = core == plane

        def finish(at):
            left, right = cut(attended, at, rows, 0), cut(got, at, rows, 0)
            own, rest = jnp.where(here, left, right), jnp.where(here, right, left)
            down = (dot_rows(own, own_down) + dot_rows(rest, rest_down)).astype(jnp.bfloat16)
            down = jnp.where(cut(columns, at, rows, 0), down, jnp.zeros_like(down))
            base = dot(own, own_out) + dot(rest, rest_out)
            return (base + adapter_scale * dot(down, ups)).astype(jnp.bfloat16)

        theirs = other_core(finish((1 - core) * rows))
        return assemble(finish(core * rows), theirs, ring.slot, core, chips)
    down = lax.psum(dot_rows(attended, downs).astype(jnp.bfloat16), "sub")
    down = jnp.where(columns, down, jnp.zeros_like(down))
    own_out = jnp.take(jnp.stack(out_own, axis=1), ring.slot, axis=1).reshape(half_rows, -1)
    rest_out = jnp.take(jnp.stack(out_rest, axis=1), ring.slot, axis=1).reshape(half_rows, -1)
    partial_out = dot(cut(attended, plane * half_rows, half_rows, 1), own_out)
    partial_out += dot(cut(attended, (1 - plane) * half_rows, half_rows, 1), rest_out)
    summed = lax.psum_scatter(
        partial_out.astype(jnp.bfloat16), "sub", scatter_dimension=1, tiled=True
    )
    return (summed.astype(jnp.float32) + adapter_scale * dot(down, ups)).astype(jnp.bfloat16)


def solution(mesh):
    planes, seq, sub = mesh.devices.shape
    cores = 2 if sub == 1 else 1
    chips = seq // cores
    if cores == 2:
        order = list(range(0, chips, 2)) + list(range(chips - 1, 0, -2))
    else:
        order = list(range(chips))
    split = Mesh(
        mesh.devices.reshape(planes, chips, cores, sub), ("groups", "chip", "core", "sub")
    )
    seq_axes = ("chip", "core")
    return jax.shard_map(
        functools.partial(shards, planes, cores, order),
        mesh=split,
        in_specs=(
            P(("groups", "chip", "core"), None),
            P(),
            P(seq_axes, "sub"),
            P(seq_axes, None, "sub"),
            P("sub", seq_axes),
            P(seq_axes, None, None),
            P(seq_axes, None, "sub"),
            P(seq_axes, None, None, "sub"),
            P(seq_axes, "sub", None),
            P(seq_axes, None, "sub"),
            P("groups"),
            P("groups"),
            P(),
        ),
        out_specs=P(("groups", "chip", "core"), "sub"),
        check_vma=False,
    )
```
